32 devices in a mesh: tm: 8 (over z, x), clips: 2 (over y), heads: 2 (over core).
Axes of the slice: x: 2, y: 2, z: 4, core: 2. Of those that a mesh axis runs over, the one named last changes fastest.
Arguments:
- tokens_big: bfloat16 [4, 16, 256, 1024], P('clips', 'tm', 'heads'), may hold values from -6 to 6
- tokens_small: bfloat16 [4, 16, 64, 1024], P('clips', 'tm', 'heads'), may hold values from -6 to 6
- mask_big: int32 [4, 16, 256], P('clips', 'tm', 'heads'), may hold values 0 or 1
- mask_small: int32 [4, 16, 64], P('clips', 'tm', 'heads'), may hold values 0 or 1
- actions_big: int32 [4, 16], P('clips', 'tm'), may hold values from 0 to 7
- actions_small: int32 [4, 16], P('clips', 'tm'), may hold values from 0 to 7
- space_qkv: bfloat16 [3, 1024, 1024], P(None, None, 'heads'), may hold values from -0.1875 to 0.1875
- space_out: bfloat16 [1024, 1024], P('heads'), may hold values from -0.5 to 0.5
- time_qkv: bfloat16 [3, 1024, 1024], P(None, None, 'heads'), may hold values from -0.1875 to 0.1875
- time_out: bfloat16 [1024, 1024], P('heads'), may hold values from -0.375 to 0.375
- ffn_in: bfloat16 [1024, 4096], P(None, 'heads'), may hold values from -0.1875 to 0.1875
- ffn_out: bfloat16 [4096, 1024], P('heads'), may hold values from -0.125 to 0.125
- ln_gain: float32 [3, 1024], replicated, may hold values from 0.1 to 1.9
- ln_bias: float32 [3, 1024], replicated, may hold values from -1 to 1
- mask_token: float32 [1024], replicated, may hold values from -6 to 6
- action_table: float32 [8, 1024], replicated, may hold values from -3 to 3
- cotangent_big: bfloat16 [4, 16, 256, 1024], P('clips', 'tm', 'heads'), may hold values from -6 to 6
- cotangent_small: bfloat16 [4, 16, 64, 1024], P('clips', 'tm', 'heads'), may hold values from -6 to 6
Outputs:
- out_big: bfloat16 [4, 16, 256, 1024], P('clips', 'tm', 'heads')
- out_small: bfloat16 [4, 16, 64, 1024], P('clips', 'tm', 'heads')
- grad_big: bfloat16 [4, 16, 256, 1024], P('clips', 'tm', 'heads')
- grad_small: bfloat16 [4, 16, 64, 1024], P('clips', 'tm', 'heads')
- grad_space_qkv: float32 [3, 1024, 1024], P(None, None, 'heads')
- grad_space_out: float32 [1024, 1024], P('heads')
- grad_time_qkv: float32 [3, 1024, 1024], P(None, None, 'heads')
- grad_time_out: float32 [1024, 1024], P('heads')
- grad_ffn_in: float32 [1024, 4096], P(None, 'heads')
- grad_ffn_out: float32 [4096, 1024], P('heads')
- grad_ln_gain: float32 [3, 1024], replicated
- grad_ln_bias: float32 [3, 1024], replicated
- grad_mask_token: float32 [1024], replicated
- grad_action_table: float32 [8, 1024], replicated
The draws below stay inside these ranges and needn't reach their ends.
All inputs are finite; a program needn't handle non-finite values. No bound on the sum of `mask_big` or of `mask_small` on one device may be relied on, other than what follows from the above.
Results may differ from the reference program's by a relative error of at most 0.024.
Values may be sent and summed in bfloat16 or wider, within the bound.
A program may use at most 320 MiB of HBM per device.

```python
import jax
import jax.numpy as jnp
from jax import lax

HEAD_DIM = 64
D = 1024
FF = 4096
ACTIONS = 8
FRAMES = 16
BIG_SIDE = 16
SMALL_SIDE = 8
BIG_CLIPS = 4
SMALL_CLIPS = 4


def set_ends(drawn, rng, smallest, high):
    longest = drawn.shape.index(max(drawn.shape))
    spots = []
    for shift in (0, 1):
        where = [jax.random.randint(jax.random.fold_in(rng, axis), (), 0, length) for axis, length in enumerate(drawn.shape)]
        where[longest] = (where[longest] + shift) % drawn.shape[longest]
        spots.append(tuple(where))
    return drawn.at[spots[0]].set(smallest).at[spots[1]].set(high)


def shard_levels(stream_key, shape, split, least, high):
    gain = 1.0
    for axis_at, blocks in split:
        steps = jax.random.uniform(jax.random.fold_in(jax.random.fold_in(stream_key, 6), axis_at), (blocks,), jnp.float32, least / len(split), high / len(split))
        gain = gain * jnp.repeat(jnp.exp(steps), shape[axis_at] // blocks).reshape((-1,) + (1,) * (len(shape) - 1 - axis_at))
    return gain


def noise(rng, dims, deviation, reach, split=(), held_as=jnp.bfloat16):
    entries = deviation * jax.random.normal(rng, dims, jnp.float32)
    if split:
        entries = entries * shard_levels(rng, dims, split, -0.22, 0.18)
    return jnp.clip(entries, -reach, reach).astype(held_as)


def setup_inputs(seed: int = 0) -> dict:
    streams_of = jax.random.split(jax.random.key(seed), 19)
    tokens_big = noise(streams_of[0], (BIG_CLIPS, FRAMES, BIG_SIDE * BIG_SIDE, D), 1.0, 6.0, ((0, 2), (1, 8), (2, 2)))
    tokens_small = noise(streams_of[1], (SMALL_CLIPS, FRAMES, SMALL_SIDE * SMALL_SIDE, D), 1.0, 6.0, ((0, 2), (1, 8), (2, 2)))
    mask_big = set_ends((jax.random.randint(streams_of[2], (BIG_CLIPS, FRAMES, BIG_SIDE * BIG_SIDE), 0, 2) < 1).astype(jnp.int32), jax.random.fold_in(streams_of[2], 1), 0, 1)
    mask_small = set_ends((jax.random.randint(streams_of[3], (SMALL_CLIPS, FRAMES, SMALL_SIDE * SMALL_SIDE), 0, 2) < 1).astype(jnp.int32), jax.random.fold_in(streams_of[3], 1), 0, 1)
    actions_big = set_ends(jax.random.randint(streams_of[4], (BIG_CLIPS, FRAMES), 0, ACTIONS), jax.random.fold_in(streams_of[4], 1), 0, ACTIONS - 1).astype(jnp.int32)
    actions_small = set_ends(jax.random.randint(streams_of[5], (SMALL_CLIPS, FRAMES), 0, ACTIONS), jax.random.fold_in(streams_of[5], 1), 0, ACTIONS - 1).astype(jnp.int32)
    space_qkv = noise(streams_of[6], (3, D, D), D ** -0.5, 0.1875, ((2, 2),))
    space_out = noise(streams_of[7], (D, D), (D // 8) ** -0.5, 0.5, ((0, 2),))
    time_qkv = noise(streams_of[8], (3, D, D), D ** -0.5, 0.1875, ((2, 2),))
    time_out = noise(streams_of[9], (D, D), (D // 4) ** -0.5, 0.375, ((0, 2),))
    ffn_in = noise(streams_of[10], (D, FF), D ** -0.5, 0.1875, ((1, 2),))
    ffn_out = noise(streams_of[11], (FF, D), (FF // 2) ** -0.5, 0.125, ((0, 2),))
    ln_gain = jnp.clip(1.0 + 0.18 * jax.random.normal(streams_of[12], (3, D), jnp.float32), 0.1, 1.9)
    ln_bias = noise(streams_of[13], (3, D), 0.2, 1.0, (), jnp.float32)
    mask_token = noise(streams_of[14], (D,), 1.0, 6.0, (), jnp.float32)
    action_table = noise(streams_of[15], (ACTIONS, D), 0.5, 3.0, (), jnp.float32)
    cotangent_big = noise(streams_of[16], (BIG_CLIPS, FRAMES, BIG_SIDE * BIG_SIDE, D), 1.0, 6.0, ((0, 2), (1, 8), (2, 2)))
    cotangent_small = noise(streams_of[17], (SMALL_CLIPS, FRAMES, SMALL_SIDE * SMALL_SIDE, D), 1.0, 6.0, ((0, 2), (1, 8), (2, 2)))
    return dict(tokens_big=tokens_big, tokens_small=tokens_small, mask_big=mask_big, mask_small=mask_small, actions_big=actions_big, actions_small=actions_small, space_qkv=space_qkv, space_out=space_out, time_qkv=time_qkv, time_out=time_out, ffn_in=ffn_in, ffn_out=ffn_out, ln_gain=ln_gain, ln_bias=ln_bias, mask_token=mask_token, action_table=action_table, cotangent_big=cotangent_big, cotangent_small=cotangent_small)


epsilon = 1e-05
masked_score = -1e+30
highest = lax.Precision.HIGHEST

@jax.custom_vjp
def low(v):
    return lax.optimization_barrier(v.astype(jnp.bfloat16)).astype(jnp.float32)

@jax.custom_vjp
def low_back(v):
    return v

def low_keep(v):
    return (low(v), None)

def low_pass(kept, grad):
    return (grad,)

def back_keep(v):
    return (v, None)

def back_low(kept, grad):
    return (low(grad),)
low.defvjp(low_keep, low_pass)
low_back.defvjp(back_keep, back_low)

def normalize(hidden, norm_gain, norm_shift):
    average = lax.optimization_barrier(jnp.mean(hidden, axis=-1, keepdims=True))
    centered = hidden - average
    inverse = lax.rsqrt(lax.optimization_barrier(jnp.mean(centered * centered, axis=-1, keepdims=True)) + epsilon)
    return centered * inverse * norm_gain + norm_shift

def clip_layer(weight_set, tokens, token_mask, actions):
    space_qkv, space_out, time_qkv, time_out, ffn_in, ffn_out, ln_gain, ln_bias, mask_token, action_table = weight_set
    frame_count, grid_size, model_width = tokens.shape
    head_count = model_width // HEAD_DIM
    score_scale = HEAD_DIM ** (-0.5)
    split_shape = (frame_count, grid_size, head_count, HEAD_DIM)
    embedded = jnp.where(token_mask[:, :, None] == 1, mask_token, tokens) + action_table[actions][:, None, :]
    first_in = low(normalize(embedded, ln_gain[0], ln_bias[0]))
    first_qkv = low(low_back(jnp.einsum('fgd,kde->kfge', first_in, space_qkv, precision=highest)))
    queries = first_qkv[0].reshape(split_shape)
    key_rows = first_qkv[1].reshape(split_shape)
    value_rows = first_qkv[2].reshape(split_shape)
    scores = low_back(jnp.einsum('fqhd,fkhd->fhqk', queries, key_rows, precision=highest) * score_scale)
    attn_probs = low(jax.nn.softmax(scores, axis=-1))
    first_mix = jnp.einsum('fhqk,fkhd->fqhd', attn_probs, value_rows, precision=highest).reshape(frame_count, grid_size, model_width)
    first_mix = low(low_back(first_mix))
    middle = embedded + low_back(jnp.einsum('fge,ed->fgd', first_mix, space_out, precision=highest))
    second_in = low(normalize(middle, ln_gain[1], ln_bias[1]))
    second_qkv = low(low_back(jnp.einsum('fgd,kde->kfge', second_in, time_qkv, precision=highest)))
    queries = second_qkv[0].reshape(split_shape)
    key_rows = second_qkv[1].reshape(split_shape)
    value_rows = second_qkv[2].reshape(split_shape)
    scores = low_back(jnp.einsum('qghd,kghd->ghqk', queries, key_rows, precision=highest) * score_scale)
    frame_order = jnp.arange(frame_count, dtype=jnp.int32)
    scores = jnp.where(frame_order[None, :] <= frame_order[:, None], scores, masked_score)
    attn_probs = low(jax.nn.softmax(scores, axis=-1))
    second_mix = jnp.einsum('ghqk,kghd->qghd', attn_probs, value_rows, precision=highest).reshape(frame_count, grid_size, model_width)
    second_mix = low(low_back(second_mix))
    after_time = middle + low_back(jnp.einsum('fge,ed->fgd', second_mix, time_out, precision=highest))
    third_in = low(normalize(after_time, ln_gain[2], ln_bias[2]))
    activation = low(jax.nn.gelu(low_back(jnp.einsum('fgd,dm->fgm', third_in, ffn_in, precision=highest))))
    return after_time + low_back(jnp.einsum('fgm,md->fgd', activation, ffn_out, precision=highest))

def reference(tokens_big, tokens_small, mask_big, mask_small, actions_big, actions_small, space_qkv, space_out, time_qkv, time_out, ffn_in, ffn_out, ln_gain, ln_bias, mask_token, action_table, cotangent_big, cotangent_small):
    weight_set = tuple((member.astype(jnp.float32) for member in (space_qkv, space_out, time_qkv, time_out, ffn_in, ffn_out, ln_gain, ln_bias, mask_token, action_table)))

    def whole_layer(layer_weights, big_in, small_in):

        def one_clip(clip_item):
            return jax.checkpoint(clip_layer)(layer_weights, clip_item[0], clip_item[1], clip_item[2])
        big_result = lax.map(one_clip, (big_in, mask_big, actions_big))
        small_result = lax.map(one_clip, (small_in, mask_small, actions_small))
        return (big_result, small_result)
    outputs, pullback = jax.vjp(whole_layer, weight_set, tokens_big.astype(jnp.float32), tokens_small.astype(jnp.float32))
    weight_grads, grad_big, grad_small = pullback((cotangent_big.astype(jnp.float32), cotangent_small.astype(jnp.float32)))
    return (outputs[0].astype(jnp.bfloat16), outputs[1].astype(jnp.bfloat16), grad_big.astype(jnp.bfloat16), grad_small.astype(jnp.bfloat16), weight_grads[0], weight_grads[1], weight_grads[2], weight_grads[3], weight_grads[4], weight_grads[5], weight_grads[6], weight_grads[7], weight_grads[8], weight_grads[9])
```

```python
import functools
import math

import jax
import jax.numpy as jnp
from jax import lax
from jax.experimental import pallas as pl
from jax.experimental.pallas import tpu as pltpu
from jax.sharding import PartitionSpec as P

HEAD_DIM = 64
PAIR = 2 * HEAD_DIM
EPSILON = 1e-05
MASKED = -1e30
SCALE = HEAD_DIM**-0.5
FF_BLOCK = 512
f32 = jnp.float32
bf16 = jnp.bfloat16
highest = lax.Precision.HIGHEST


def nn(a, b):
    return lax.dot_general(a, b, (((1,), (0,)), ((), ())), preferred_element_type=f32)


def nt(a, b):
    return lax.dot_general(a, b, (((1,), (1,)), ((), ())), preferred_element_type=f32)


def tn(a, b):
    return lax.dot_general(a, b, (((0,), (0,)), ((), ())), preferred_element_type=f32)


def standardize(hidden):
    average = jnp.mean(hidden, axis=-1, keepdims=True)
    centered = hidden - average
    inverse = lax.rsqrt(jnp.mean(centered * centered, axis=-1, keepdims=True) + EPSILON)
    return centered * inverse, inverse


def normalize_back(upstream, standard, inverse, gain):
    scaled = upstream * gain
    adjusted = scaled - jnp.mean(scaled, axis=-1, keepdims=True)
    adjusted = adjusted - standard * jnp.mean(scaled * standard, axis=-1, keepdims=True)
    return adjusted * inverse


def head_lanes(dtype):
    lane = lax.broadcasted_iota(jnp.int32, (1, PAIR), 1)
    first = (lane < HEAD_DIM).astype(dtype)
    return first, 1 - first


def causal_mask(size, group):
    row = lax.broadcasted_iota(jnp.int32, (size, size), 0)
    col = lax.broadcasted_iota(jnp.int32, (size, size), 1)
    same = lax.rem(row, group) == lax.rem(col, group)
    return same, row, col


def attend_kernel(segments, group, qkv_ref, mix_ref):
    sel = head_lanes(bf16)
    keep = None
    if group:
        same, row, col = causal_mask(segments[0][1], group)
        keep = jnp.logical_and(same, col <= row)
    for start, size in segments:
        rows = pl.ds(start, size)
        queries, keys, values = qkv_ref[0, rows, :], qkv_ref[1, rows, :], qkv_ref[2, rows, :]
        total = jnp.zeros((size, PAIR), f32)
        for lanes in sel:
            scores = nt(queries * lanes, keys) * SCALE
            if group:
                scores = jnp.where(keep, scores, MASKED)
            exponent = jnp.exp(scores - jnp.max(scores, axis=-1, keepdims=True))
            probs = exponent * (1.0 / jnp.sum(exponent, axis=-1, keepdims=True))
            total = total + nn(probs.astype(bf16), values * lanes)
        mix_ref[rows, :] = total.astype(bf16)


def attend_back_kernel(segments, group, qkv_ref, up_ref, grad_ref):
    sel = head_lanes(bf16)
    keep = None
    if group:
        same, row, col = causal_mask(segments[0][1], group)
        keep = jnp.logical_and(same, row <= col)
    for start, size in segments:
        rows = pl.ds(start, size)
        queries, keys, values = qkv_ref[0, rows, :], qkv_ref[1, rows, :], qkv_ref[2, rows, :]
        upstream = up_ref[rows, :]
        query_grad = jnp.zeros((size, PAIR), f32)
        key_grad = jnp.zeros((size, PAIR), f32)
        value_grad = jnp.zeros((size, PAIR), f32)
        for lanes in sel:
            some_queries = queries * lanes
            some_upstream = upstream * lanes
            scores = nt(keys, some_queries) * SCALE
            if group:
                scores = jnp.where(keep, scores, MASKED)
            exponent = jnp.exp(scores - jnp.max(scores, axis=0, keepdims=True))
            probs = exponent * (1.0 / jnp.sum(exponent, axis=0, keepdims=True))
            prob_grad = nt(values, some_upstream)
            inner = jnp.sum(probs * prob_grad, axis=0, keepdims=True)
            score_grad = (probs * (prob_grad - inner)).astype(bf16)
            value_grad = value_grad + nn(probs.astype(bf16), some_upstream)
            key_grad = key_grad + nn(score_grad, some_queries)
            query_grad = query_grad + tn(score_grad, keys * lanes)
        grad_ref[0, rows, :] = (query_grad * SCALE).astype(bf16)
        grad_ref[1, rows, :] = (key_grad * SCALE).astype(bf16)
        grad_ref[2, rows, :] = value_grad.astype(bf16)


def attend(qkv, segments, group):
    unused, count, width = qkv.shape
    area = sum(size * size for unused, size in segments)
    return pl.pallas_call(
        functools.partial(attend_kernel, segments, group),
        grid=(width // PAIR,),
        in_specs=[pl.BlockSpec((3, count, PAIR), lambda i: (0, 0, i))],
        out_specs=pl.BlockSpec((count, PAIR), lambda i: (0, i)),
        out_shape=jax.ShapeDtypeStruct((count, width), bf16),
        cost_estimate=pl.CostEstimate(
            flops=area * 8 * width, bytes_accessed=8 * count * width, transcendentals=area * width // HEAD_DIM
        ),
        name="attend",
    )(qkv)


def attend_back(qkv, upstream, segments, group):
    unused, count, width = qkv.shape
    area = sum(size * size for unused, size in segments)
    return pl.pallas_call(
        functools.partial(attend_back_kernel, segments, group),
        grid=(width // PAIR,),
        in_specs=[
            pl.BlockSpec((3, count, PAIR), lambda i: (0, 0, i)),
            pl.BlockSpec((count, PAIR), lambda i: (0, i)),
        ],
        out_specs=pl.BlockSpec((3, count, PAIR), lambda i: (0, 0, i)),
        out_shape=jax.ShapeDtypeStruct((3, count, width), bf16),
        cost_estimate=pl.CostEstimate(
            flops=area * 20 * width, bytes_accessed=14 * count * width, transcendentals=area * width // HEAD_DIM
        ),
        name="attend_back",
    )(qkv, upstream)


def ffn_kernel(x_ref, up_ref, in_ref, out_ref, y_ref, back_ref, grad_in_ref, grad_out_ref, x_turned, up_turned):
    step = pl.program_id(0)

    @pl.when(step == 0)
    def _():
        x_turned[...] = x_ref[...].T
        up_turned[...] = up_ref[...].T
        y_ref[...] = jnp.zeros_like(y_ref)
        back_ref[...] = jnp.zeros_like(back_ref)

    rows = x_ref[...]
    upstream = up_ref[...]
    first = in_ref[...]
    second = out_ref[...]
    pre_act = nn(rows, first)
    square = pre_act * pre_act
    slope = math.sqrt(2 / math.pi)
    tanh = jnp.tanh(slope * (pre_act + 0.044715 * (pre_act * square)))
    half = 0.5 * (1.0 + tanh)
    activation = (pre_act * half).astype(bf16)
    derivative = half + (0.5 * slope) * pre_act * (1.0 - tanh * tanh) * (1.0 + 0.134145 * square)
    pre_grad = (nt(upstream, second) * derivative).astype(bf16)
    y_ref[...] += nn(activation, second)
    back_ref[...] += nt(pre_grad, first)
    grad_in_ref[...] = nn(x_turned[...], pre_grad).astype(bf16)
    grad_out_ref[...] = nn(up_turned[...], activation).astype(bf16)


def ffn(rows, upstream, first, second):
    count, width = rows.shape
    hidden = first.shape[1]
    block = min(FF_BLOCK, hidden)
    whole = pl.BlockSpec((count, width), lambda i: (0, 0))
    columns = pl.BlockSpec((width, block), lambda i: (0, i))
    return pl.pallas_call(
        ffn_kernel,
        grid=(hidden // block,),
        in_specs=[whole, whole, columns, pl.BlockSpec((block, width), lambda i: (i, 0))],
        out_specs=[whole, whole, columns, columns],
        out_shape=[
            jax.ShapeDtypeStruct((count, width), f32),
            jax.ShapeDtypeStruct((count, width), f32),
            jax.ShapeDtypeStruct((width, hidden), bf16),
            jax.ShapeDtypeStruct((width, hidden), bf16),
        ],
        scratch_shapes=[pltpu.VMEM((width, count), bf16), pltpu.VMEM((width, count), bf16)],
        cost_estimate=pl.CostEstimate(
            flops=12 * count * width * hidden,
            bytes_accessed=8 * width * hidden + 12 * count * width,
            transcendentals=count * hidden,
        ),
        name="ffn",
    )(rows, upstream, first, second)


def swap(value, axis, bit):
    size = lax.axis_size(axis)
    return lax.ppermute(value, axis, [(i, i ^ (1 << bit)) for i in range(size)])


def bit_of(axis, bit):
    return lax.rem(lax.div(lax.axis_index(axis), jnp.int32(1 << bit)), jnp.int32(2))


def stage_orders():
    time_bits = [("tm", b) for b in range(lax.axis_size("tm").bit_length() - 1)]
    clip_bits = [("clips", b) for b in range(lax.axis_size("clips").bit_length() - 1)]
    near, far = time_bits[:1], time_bits[1:]
    return (near + clip_bits + far, clip_bits + near + far, far + near + clip_bits)


def scatter_sum(buffer, order):
    for axis, bit in order:
        mine = bit_of(axis, bit)
        halves = buffer.reshape((2, buffer.shape[0] // 2) + buffer.shape[1:])
        kept = lax.dynamic_index_in_dim(halves, mine, 0, keepdims=False)
        sent = lax.dynamic_index_in_dim(halves, 1 - mine, 0, keepdims=False)
        got = swap(sent, axis, bit)
        buffer = (kept.astype(f32) + got.astype(f32)).astype(bf16)
    return buffer


def gather_back(shard, order):
    for axis, bit in reversed(order):
        got = swap(shard, axis, bit)
        low = bit_of(axis, bit) == 0
        shard = jnp.concatenate([jnp.where(low, shard, got), jnp.where(low, got, shard)], axis=0)
    return shard


def total_sum(buffer):
    orders = stage_orders()[0]
    for axis, bit in [("heads", 0)] + orders:
        buffer = buffer + swap(buffer, axis, bit)
    return buffer


def thirds(buffer):
    rows = buffer.shape[0]
    cut = rows * 3 // 8
    return buffer[:cut], buffer[cut : 2 * cut], buffer[2 * cut :]


def reduce_parts(parts):
    return [scatter_sum(part, order) for part, order in zip(parts, stage_orders())]


def gather_parts(shards):
    return [gather_back(shard, order) for shard, order in zip(shards, stage_orders())]


def per_device(
    tokens_big,
    tokens_small,
    mask_big,
    mask_small,
    actions_big,
    actions_small,
    space_qkv,
    space_out,
    time_qkv,
    time_out,
    ffn_in,
    ffn_out,
    ln_gain,
    ln_bias,
    mask_token,
    action_table,
    cotangent_big,
    cotangent_small,
):
    clips, frames, big, width = tokens_big.shape
    small = tokens_small.shape[2]
    devices = lax.axis_size("tm")
    core = lax.axis_index("heads")
    group = 2 * small // devices
    per_frame = 2 * (big + small)
    count = frames * per_frame
    blocks = per_frame // devices // group
    all_frames = devices * frames
    half_width = space_qkv.shape[2]

    def partner(value):
        return swap(value, "heads", 0)

    space_qkv_pair = (space_qkv, partner(space_qkv))
    space_out_pair = (space_out, partner(space_out))
    time_qkv_pair = (time_qkv, partner(time_qkv))
    time_out_pair = (time_out, partner(time_out))
    ffn_in_pair = (ffn_in, partner(ffn_in))
    ffn_out_pair = (ffn_out, partner(ffn_out))

    def to_frames(own, other):
        own_big, own_small = own[:, :big], own[:, big:]
        other_big, other_small = other[:, :big], other[:, big:]
        return jnp.concatenate([own_big, other_big, own_small, other_small], axis=1)

    def from_frames(rows):
        own = jnp.concatenate([rows[:, :big], rows[:, 2 * big : 2 * big + small]], axis=1)
        other = jnp.concatenate([rows[:, big : 2 * big], rows[:, 2 * big + small :]], axis=1)
        return own, other

    def pick(big_rows, small_rows, index):
        return jnp.concatenate(
            [
                lax.dynamic_index_in_dim(big_rows, index, 0, keepdims=False),
                lax.dynamic_index_in_dim(small_rows, index, 0, keepdims=False),
            ],
            axis=1,
        )

    def gather_clip(big_rows, small_rows):
        other = partner(pick(big_rows, small_rows, 1 - core))
        return to_frames(pick(big_rows, small_rows, core), other)

    def to_positions(rows):
        rows = rows.reshape(frames, per_frame, width)
        large = rows[:, : 2 * big].reshape(frames, 2, devices, big // devices // group, group, width)
        large = large.transpose(2, 1, 3, 0, 4, 5).reshape(devices, blocks - 1, frames, group, width)
        little = rows[:, 2 * big :].reshape(frames, 2, devices, group // 2, width)
        little = little.transpose(2, 0, 1, 3, 4).reshape(devices, 1, frames, group, width)
        packed = jnp.concatenate([large, little], axis=1)
        got = lax.all_to_all(packed, "tm", 0, 0)
        return got.transpose(1, 0, 2, 3, 4).reshape(count, width)

    def to_own_frames(rows):
        rows = rows.reshape(blocks, devices, frames, group, width).transpose(1, 0, 2, 3, 4)
        got = lax.all_to_all(rows, "tm", 0, 0)
        large = got[:, : blocks - 1].reshape(devices, 2, big // devices // group, frames, group, width)
        large = large.transpose(3, 1, 0, 2, 4, 5).reshape(frames, 2 * big, width)
        little = got[:, blocks - 1].reshape(devices, frames, 2, group // 2, width)
        little = little.transpose(1, 2, 0, 3, 4).reshape(frames, 2 * small, width)
        return jnp.concatenate([large, little], axis=1)

    space_segments = []
    for frame in range(frames):
        space_segments += [(frame * per_frame, 2 * big), (frame * per_frame + 2 * big, 2 * small)]
    space_segments = tuple(space_segments)
    time_segments = tuple((b * all_frames * group, all_frames * group) for b in range(blocks))

    upstream = to_positions(gather_clip(cotangent_big, cotangent_small))

    def embed(tokens, token_mask, actions):
        ids = jnp.arange(action_table.shape[0], dtype=jnp.int32)
        onehot = (actions[:, :, None] == ids).astype(f32)
        rows = lax.dot_general(onehot, action_table, (((2,), (0,)), ((), ())), precision=highest)
        masked = jnp.where(token_mask[:, :, :, None] == 1, mask_token, tokens.astype(f32))
        return (masked + rows[:, :, None, :]).astype(bf16)

    embedded = gather_clip(
        embed(tokens_big, mask_big, actions_big), embed(tokens_small, mask_small, actions_small)
    ).reshape(count, width)

    def norm(rows, index):
        standard, unused = standardize(rows.astype(f32))
        return (standard * ln_gain[index] + ln_bias[index]).astype(bf16)

    def project(rows, weight):
        return lax.dot_general(rows, weight, (((1,), (1,)), ((), ())), preferred_element_type=f32).astype(bf16).transpose(1, 0, 2)

    def qkv_of(rows, pair):
        return [project(rows, weight) for weight in pair]

    first_in = norm(embedded, 0)
    first_qkv = qkv_of(first_in, space_qkv_pair)
    first_mix = [attend(member, space_segments, 0) for member in first_qkv]
    middle = (
        embedded.astype(f32) + nn(first_mix[0], space_out_pair[0]) + nn(first_mix[1], space_out_pair[1])
    ).astype(bf16)
    middle = to_positions(middle)

    second_in = norm(middle, 1)
    second_qkv = qkv_of(second_in, time_qkv_pair)
    second_mix = [attend(member, time_segments, group) for member in second_qkv]
    after_time = (
        middle.astype(f32) + nn(second_mix[0], time_out_pair[0]) + nn(second_mix[1], time_out_pair[1])
    )

    third_in = norm(after_time, 2)
    other_y, other_back, other_in_grad, other_out_grad = ffn(third_in, upstream, ffn_in_pair[1], ffn_out_pair[1])
    own_y, own_back, own_in_grad, own_out_grad = ffn(third_in, upstream, ffn_in_pair[0], ffn_out_pair[0])

    def join(own, other):
        return (own.astype(f32) + partner(other).astype(f32)).astype(bf16)

    grad_ffn_in = join(own_in_grad, other_in_grad)
    grad_ffn_out = join(own_out_grad, other_out_grad)
    cut = width * 3 // 4
    ffn_parts = [
        grad_ffn_in[:cut],
        grad_ffn_out[:cut],
        jnp.concatenate([grad_ffn_in[cut:], grad_ffn_out[cut:]], axis=0),
    ]
    ffn_shards = reduce_parts(ffn_parts)

    out = to_own_frames((after_time + other_y + own_y).astype(bf16))

    third_back = other_back + own_back
    third_standard, third_inverse = standardize(after_time)
    grad_after = upstream.astype(f32) + normalize_back(third_back, third_standard, third_inverse, ln_gain[2])

    def qkv_back(rows_in, qkv_pair, mix_pair, weight_pair, out_pair, gradient, segments, mask_group):
        low_gradient = gradient.astype(bf16)
        back = 0.0
        halves = []
        for which in (1, 0):
            mix_grad = nt(low_gradient, out_pair[which]).astype(bf16)
            qkv_grad = attend_back(qkv_pair[which], mix_grad, segments, mask_group)
            back = back + lax.dot_general(
                qkv_grad, weight_pair[which], (((0, 2), (0, 2)), ((), ())), preferred_element_type=f32
            )
            grad_qkv = [tn(rows_in, qkv_grad[j]).astype(bf16) for j in range(3)]
            grad_out = tn(mix_pair[which], low_gradient).astype(bf16)
            pieces = [member.reshape(-1, half_width, half_width) for member in grad_qkv]
            pieces += [grad_out[None, :, :half_width], grad_out[None, :, half_width:]]
            halves.append(jnp.concatenate(pieces, axis=0))
        joined = join(halves[1], halves[0])
        return back, joined.reshape(-1, half_width)

    second_back, time_grads = qkv_back(
        second_in, second_qkv, second_mix, time_qkv_pair, time_out_pair, grad_after, time_segments, group
    )
    second_standard, second_inverse = standardize(middle.astype(f32))
    grad_middle = grad_after + normalize_back(second_back, second_standard, second_inverse, ln_gain[1])
    grad_middle = to_own_frames(grad_middle.astype(bf16)).reshape(count, width)
    time_shards = reduce_parts(thirds(time_grads))

    first_back, space_grads = qkv_back(
        first_in,
        first_qkv,
        first_mix,
        space_qkv_pair,
        space_out_pair,
        grad_middle,
        space_segments,
        0,
    )
    first_standard, first_inverse = standardize(embedded.astype(f32))
    grad_embedded = grad_middle.astype(f32) + normalize_back(
        first_back, first_standard, first_inverse, ln_gain[0]
    )
    space_shards = reduce_parts(thirds(space_grads))

    grad_frames = grad_embedded.reshape(frames, per_frame, width)

    def placed(rows):
        own, other = from_frames(rows)
        got = partner(other)
        low = core == 0
        first = jnp.where(low, own, got)
        second = jnp.where(low, got, own)
        both = jnp.stack([first, second])
        return both[:, :, :big], both[:, :, big:]

    out_big, out_small = placed(out)
    grad_big, grad_small = placed(grad_frames.astype(bf16))
    masked_big = mask_big[:, :, :, None] == 1
    masked_small = mask_small[:, :, :, None] == 1
    mask_grad = jnp.sum(jnp.where(masked_big, grad_big.astype(f32), 0.0), axis=(0, 1, 2)) + jnp.sum(
        jnp.where(masked_small, grad_small.astype(f32), 0.0), axis=(0, 1, 2)
    )
    grad_big = jnp.where(masked_big, jnp.zeros_like(grad_big), grad_big)
    grad_small = jnp.where(masked_small, jnp.zeros_like(grad_small), grad_small)

    ids = jnp.arange(action_table.shape[0], dtype=jnp.int32)

    def table_part(actions, rows):
        ours = lax.dynamic_index_in_dim(actions, core, 0, keepdims=False)
        onehot = (ours[:, None] == ids).astype(f32)
        return lax.dot_general(
            onehot, jnp.sum(rows, axis=1), (((0,), (0,)), ((), ())), precision=highest
        )

    table_grad = table_part(actions_big, grad_frames[:, : 2 * big]) + table_part(
        actions_small, grad_frames[:, 2 * big :]
    )
    gains = [
        jnp.sum(back * standard, axis=0)
        for back, standard in (
            (first_back, first_standard),
            (second_back, second_standard),
            (third_back, third_standard),
        )
    ]
    shifts = [jnp.sum(back, axis=0) for back in (first_back, second_back, third_back)]
    totals = total_sum(jnp.concatenate([jnp.stack(gains + shifts + [mask_grad]), table_grad], axis=0))

    in_part, out_part, mixed_part = gather_parts(ffn_shards)
    rest = width - cut
    full_in = jnp.concatenate([in_part, mixed_part[:rest]], axis=0).astype(f32)
    full_out = jnp.concatenate([out_part, mixed_part[rest:]], axis=0).T.astype(f32)

    def unpack(shards):
        full = jnp.concatenate(gather_parts(shards), axis=0).astype(f32)
        full = full.reshape(-1, half_width, half_width)
        qkv = full[: full.shape[0] - 2].reshape(space_qkv.shape)
        return qkv, jnp.concatenate([full[-2], full[-1]], axis=1)

    full_time_qkv, full_time_out = unpack(time_shards)
    full_space_qkv, full_space_out = unpack(space_shards)
    return (
        out_big,
        out_small,
        grad_big,
        grad_small,
        full_space_qkv,
        full_space_out,
        full_time_qkv,
        full_time_out,
        full_in,
        full_out,
        totals[0:3],
        totals[3:6],
        totals[6],
        totals[7:],
    )


def solution(mesh):
    rows = P("clips", "tm", "heads", None)
    masks = P("clips", "tm", "heads")
    actions = P("clips", "tm")
    last = P(None, None, "heads")
    first = P("heads", None)
    placed = (rows, rows, masks, masks, actions, actions)
    placed += (last, first, last, first, P(None, "heads"), first)
    placed += (P(), P(), P(), P(), rows, rows)
    results = (rows, rows, rows, rows, last, first, last, first, P(None, "heads"), first)
    results += (P(), P(), P(), P())
    return jax.shard_map(per_device, mesh=mesh, in_specs=placed, out_specs=results, check_vma=False)
```
